256 devices in a mesh: dp: 4 (over z_hi, core), seq: 64 (over z_lo, y, x).
Axes of the slice: x: 4, y: 4, z: 8 (z_hi: 2, z_lo: 4; z = z_hi * 4 + z_lo), core: 2. Of those that a mesh axis runs over, the one named last changes fastest.
Arguments:
- inputs: bfloat16 [4, 128, 262144], P('dp', None, 'seq'), may hold values from -6 to 6
- grad_out: bfloat16 [4, 128, 262144], P('dp', None, 'seq'), may hold values from -6 to 6
- factor_one: bfloat16 [512, 512], replicated, may hold values from -0.25 to 0.25
- factor_two: bfloat16 [512, 512], replicated, may hold values from -0.25 to 0.25
- factor_three: bfloat16 [512, 512], replicated, may hold values from -0.25 to 0.25
- factor_four: bfloat16 [512, 512], replicated, may hold values from -0.25 to 0.25
- twiddle_in: bfloat16 [512, 512], P('seq'), may hold values from 0.5 to 1.5
- twiddle_out: bfloat16 [512, 512], P('seq'), may hold values from 0.5 to 1.5
- filter_freq: bfloat16 [128, 512, 512], P(None, 'seq'), may hold values from -6 to 6
- skip_gain: float32 [128], replicated, may hold values from 0.5 to 1.5
Outputs:
- outputs: bfloat16 [4, 128, 262144], P('dp', None, 'seq')
- filter_grad: bfloat16 [128, 512, 512], P(None, 'seq')
The draws below stay inside these ranges and needn't reach their ends.
All inputs are finite; a program needn't handle non-finite values.
Results may differ from the reference program's by a relative error of at most 0.013.
Values may be sent and summed in bfloat16 or wider, within the bound.
No kernel may reach another device: no remote copies, remote signals or barrier semaphores. Data moves between devices by JAX's collectives and lax.ppermute only.
A program may use at most 64 MiB of HBM per device.

```python
import jax
import jax.numpy as jnp
from jax import lax

P_SIZE = 512
Q = 512
C = 128
L = 262144
BATCH = 4
N_DP = 4


def level_of(key, dims, pieces, low, largest):
    loudness = 1.0
    for position, blocks in pieces:
        steps = jax.random.uniform(jax.random.fold_in(jax.random.fold_in(key, 6), position), (blocks,), jnp.float32, low / len(pieces), largest / len(pieces))
        loudness = loudness * jnp.repeat(jnp.exp(steps), dims[position] // blocks).reshape((-1,) + (1,) * (len(dims) - 1 - position))
    return loudness


def gaussian(own_key, shape, scale, reach, pieces=(), kind=jnp.bfloat16):
    drawn = scale * jax.random.normal(own_key, shape, jnp.float32)
    if pieces:
        drawn = drawn * level_of(own_key, shape, pieces, -0.22, 0.18)
    return jnp.clip(drawn, -reach, reach).astype(kind)


def setup_inputs(seed: int = 0) -> dict:
    arg_keys = jax.random.split(jax.random.key(seed), 11)
    inputs = gaussian(arg_keys[0], (BATCH, C, L), 1.0, 6.0, ((0, 4), (2, 64)))
    grad_out = gaussian(arg_keys[1], (BATCH, C, L), 1.0, 6.0, ((0, 4), (2, 64)))
    factor_one = gaussian(arg_keys[2], (Q, Q), Q ** -0.5, 0.25)
    factor_two = gaussian(arg_keys[3], (P_SIZE, P_SIZE), P_SIZE ** -0.5, 0.25)
    factor_three = gaussian(arg_keys[4], (P_SIZE, P_SIZE), P_SIZE ** -0.5, 0.25)
    factor_four = gaussian(arg_keys[5], (Q, Q), Q ** -0.5, 0.25)
    twiddle_in = jnp.clip(0.5 + 1.0 * jax.random.uniform(arg_keys[6], (P_SIZE, Q), jnp.float32) ** level_of(arg_keys[6], (P_SIZE, Q), ((0, 64),), -0.2, 0.2), 0.5, 1.5).astype(jnp.bfloat16)
    twiddle_out = jnp.clip(0.5 + 1.0 * jax.random.uniform(arg_keys[7], (Q, P_SIZE), jnp.float32) ** level_of(arg_keys[7], (Q, P_SIZE), ((0, 64),), -0.2, 0.2), 0.5, 1.5).astype(jnp.bfloat16)
    filter_freq = gaussian(arg_keys[8], (C, Q, P_SIZE), 1.0, 6.0, ((1, 64),))
    skip_gain = jnp.clip(jax.random.uniform(arg_keys[9], (C,), jnp.float32, 0.5, 1.5), 0.5, 1.5)
    return dict(inputs=inputs, grad_out=grad_out, factor_one=factor_one, factor_two=factor_two, factor_three=factor_three, factor_four=factor_four, twiddle_in=twiddle_in, twiddle_out=twiddle_out, filter_freq=filter_freq, skip_gain=skip_gain)


def rounded(values):
    return lax.optimization_barrier(values.astype(jnp.bfloat16)).astype(jnp.float32)


def product(form, left, right):
    return jnp.einsum(form, left, right, precision=lax.Precision.HIGHEST)


def reference(inputs, grad_out, factor_one, factor_two, factor_three, factor_four, twiddle_in, twiddle_out, filter_freq, skip_gain):
    width = 8
    groups = C // width
    one = factor_one.astype(jnp.float32)
    two = factor_two.astype(jnp.float32)
    three = factor_three.astype(jnp.float32)
    four = factor_four.astype(jnp.float32)
    twist_in = twiddle_in.astype(jnp.float32)
    twist_out = twiddle_out.astype(jnp.float32)

    def one_group(index):
        start = (index * width).astype(jnp.int32)
        signal = lax.dynamic_slice_in_dim(inputs, start, width, 1).astype(jnp.float32).reshape(N_DP, width, P_SIZE, Q)
        upstream = lax.dynamic_slice_in_dim(grad_out, start, width, 1).astype(jnp.float32).reshape(N_DP, width, P_SIZE, Q)
        kernel = lax.dynamic_slice_in_dim(filter_freq, start, width, 0).astype(jnp.float32)
        gains = lax.dynamic_slice_in_dim(skip_gain, start, width, 0).astype(jnp.float32)
        twisted = rounded(product("bcpq,qk->bcpk", signal, one) * twist_in)
        spread = rounded(product("bcpk,pj->bckj", twisted, two))
        filtered = rounded(spread * kernel)
        mixed = rounded(product("bckj,ji->bcki", filtered, three) * twist_out)
        final = product("bcki,km->bcim", mixed, four) + gains[None, :, None, None] * signal
        final = final.astype(jnp.bfloat16).reshape(N_DP, width, P_SIZE * Q)
        back = rounded(product("bcim,km->bcki", upstream, four))
        back = rounded(back * twist_out)
        grads = product("bcki,ji->bckj", back, three)
        terms = rounded(spread * grads)
        total = jnp.sum(terms, axis=0).astype(jnp.bfloat16)
        return final, total

    finals, totals = lax.map(one_group, jnp.arange(groups, dtype=jnp.int32))
    outputs = jnp.transpose(finals, (1, 0, 2, 3)).reshape(N_DP, C, P_SIZE * Q)
    filter_grad = totals.reshape(C, Q, P_SIZE)
    return outputs, filter_grad
```

```python
import jax
import jax.numpy as jnp
from jax import lax
from jax.experimental import pallas as pl
from jax.experimental.pallas import tpu as pltpu
from jax.sharding import PartitionSpec as P

F32 = jnp.float32
BF16 = jnp.bfloat16
LANES = 128
ROWS = 8
WIDTH = 512
Z_LO = 4
YX = 16
PART = WIDTH // Z_LO
MSG = ROWS * ROWS
PARAMS = pltpu.CompilerParams(vmem_limit_bytes=32 * 1024 * 1024)

NT = (((1,), (1,)), ((), ()))
NN = (((1,), (0,)), ((), ()))
TN = (((0,), (0,)), ((), ()))


def dot(left, right, dims=NN):
    return lax.dot_general(left, right, dims, preferred_element_type=F32)


def my_z():
    return lax.axis_index("seq") // YX


def my_core():
    return lax.axis_index("dp") % 2


def part(z, e):
    return pl.ds(pl.multiple_of((z ^ e) * PART, PART), PART)


def struct(shape, dtype=BF16):
    return jax.ShapeDtypeStruct(shape, dtype)


def vmem(n):
    return [pl.BlockSpec(memory_space=pltpu.VMEM) for _ in range(n)]


def call(body, outs, scratch, *args):
    return pl.pallas_call(
        body,
        out_shape=outs,
        in_specs=vmem(len(args)),
        out_specs=jax.tree.map(lambda _: pl.BlockSpec(memory_space=pltpu.VMEM), outs),
        scratch_shapes=scratch,
        compiler_params=PARAMS,
    )(*args)


BLOCKS = [struct((YX, MSG, LANES))] * Z_LO


def rows_out(weight_scr, x_ref, twist, scr, out_refs):
    for pair in range(ROWS // 2):
        left = x_ref[:, (2 * pair) * WIDTH : (2 * pair + 1) * WIDTH]
        right = x_ref[:, (2 * pair + 1) * WIDTH : (2 * pair + 2) * WIDTH]
        both = dot(weight_scr[...], jnp.concatenate([left, right], axis=0), NT)
        for half in range(2):
            r = 2 * pair + half
            value = both[:, half * LANES : (half + 1) * LANES]
            if twist is not None:
                value = value * twist[:, r : r + 1]
            scr[pl.ds(r, WIDTH, stride=ROWS), :] = value
    step = WIDTH * ROWS // Z_LO
    for e, out in enumerate(out_refs):
        out[...] = scr[e * step : (e + 1) * step, :].astype(BF16).reshape(YX, MSG, LANES)


def first_body(x_ref, f_ref, tw_ref, o0, o1, o2, o3, fscr, scr):
    z = my_z()
    twist = []
    for e in range(Z_LO):
        fscr[e * PART : (e + 1) * PART, :] = f_ref[:, part(z, e)].T
        twist.append(tw_ref[:, part(z, e)].astype(F32).T)
    rows_out(fscr, x_ref, jnp.concatenate(twist, axis=0), scr, (o0, o1, o2, o3))


def back_body(x_ref, f_ref, o0, o1, o2, o3, fscr, scr):
    z = my_z()
    for e in range(Z_LO):
        fscr[e * PART : (e + 1) * PART, :] = f_ref[part(z, e), :]
    rows_out(fscr, x_ref, None, scr, (o0, o1, o2, o3))


def columns(recv_ref, pair):
    got = [[], []]
    for e in range(Z_LO):
        block = recv_ref[:, e, pair * 16 : (pair + 1) * 16, :].astype(F32)
        block = block.reshape(YX, 2, ROWS, LANES)
        for half in range(2):
            got[half].append(block[:, half].reshape(PART, LANES))
    return [jnp.concatenate(parts, axis=0) for parts in got]


def twist_columns(tw_ref, z):
    return jnp.concatenate(
        [tw_ref[:, part(z, e)].astype(F32).T for e in range(Z_LO)], axis=0
    )


def middle_body(u_ref, f2t_ref, f3t_ref, tw_ref, filt_ref, zt_ref, o0, o1, o2, o3, f2s, f3s):
    z = my_z()
    for e in range(Z_LO):
        f2s[:, e * PART : (e + 1) * PART] = f2t_ref[:, part(z, e)]
        f3s[e * PART : (e + 1) * PART, :] = f3t_ref[part(z, e), :]
    twist = twist_columns(tw_ref, z)
    for pair in range(ROWS // 2):
        k = 2 * pair
        cols = columns(u_ref, pair)
        rhs = jnp.concatenate([c.astype(BF16) for c in cols], axis=1)
        spread = dot(f2s[...], rhs).astype(BF16)
        zt_ref[k] = spread[:, :LANES]
        zt_ref[k + 1] = spread[:, LANES:]
        filt = jnp.concatenate([filt_ref[k], filt_ref[k + 1]], axis=1)
        filtered = (spread.astype(F32) * filt.astype(F32)).astype(BF16)
        third = dot(f3s[...], filtered)
        first = third[:, :LANES] * twist[:, k : k + 1]
        second = third[:, LANES:] * twist[:, k + 1 : k + 2]
        shaped = jnp.concatenate(
            [first.reshape(Z_LO * YX, ROWS, LANES), second.reshape(Z_LO * YX, ROWS, LANES)],
            axis=1,
        ).astype(BF16)
        for e, out in enumerate((o0, o1, o2, o3)):
            out[:, pair * 16 : (pair + 1) * 16, :] = shaped[e * YX : (e + 1) * YX]


def grad_body(d_ref, f3_ref, tw_ref, zt_ref, keep_ref, send_ref, f3s):
    z = my_z()
    core = my_core()
    half = WIDTH // 2
    mine = pl.ds(pl.multiple_of(core * half, half), half)
    other = pl.ds(pl.multiple_of((1 - core) * half, half), half)
    for e in range(Z_LO):
        f3s[:half, e * PART : (e + 1) * PART] = f3_ref[mine, part(z, e)]
        f3s[half:, e * PART : (e + 1) * PART] = f3_ref[other, part(z, e)]
    twist = twist_columns(tw_ref, z)
    for pair in range(ROWS // 2):
        k = 2 * pair
        cols = columns(d_ref, pair)
        rhs = jnp.concatenate(
            [(cols[h] * twist[:, k + h : k + h + 1]).astype(BF16) for h in range(2)], axis=1
        )
        grads = dot(f3s[...], rhs)
        for h in range(2):
            value = grads[:, h * LANES : (h + 1) * LANES]
            keep_ref[k + h] = (zt_ref[k + h, mine, :].astype(F32) * value[:half]).astype(BF16)
            send_ref[k + h] = (zt_ref[k + h, other, :].astype(F32) * value[half:]).astype(BF16)


def last_body(s_ref, f_ref, x_ref, g_ref, o_ref, fscr, scr):
    z = my_z()
    step = YX * MSG
    for e in range(Z_LO):
        fscr[e * PART : (e + 1) * PART, :] = f_ref[part(z, e), :]
        scr[e * step : (e + 1) * step, :] = s_ref[:, e].astype(F32).reshape(step, LANES)
    gains = g_ref[...]
    for r in range(ROWS):
        rows = scr[pl.ds(r, WIDTH, stride=ROWS), :].astype(BF16)
        fourth = dot(rows, fscr[...], TN)
        signal = x_ref[:, r * WIDTH : (r + 1) * WIDTH].astype(F32)
        o_ref[:, r * WIDTH : (r + 1) * WIDTH] = (fourth + gains * signal).astype(BF16)


def add_body(a_ref, b_ref, o_ref):
    o_ref[...] = (a_ref[...].astype(F32) + b_ref[...].astype(F32)).astype(BF16)


def total_body(a_ref, b_ref, o_ref, scr):
    for side in range(2):
        span = slice(side * LANES, (side + 1) * LANES)
        for k in range(ROWS):
            total = a_ref[k, span, :].astype(F32) + b_ref[k, span, :].astype(F32)
            scr[pl.ds(k, LANES, stride=ROWS), :] = total.T
        o_ref[:, span] = scr[...].astype(BF16)


def join_body(a_ref, b_ref, o_ref):
    core = my_core()
    half = WIDTH // 2
    o_ref[:, pl.ds(pl.multiple_of(core * half, half), half)] = a_ref[...]
    o_ref[:, pl.ds(pl.multiple_of((1 - core) * half, half), half)] = b_ref[...]


def across_z(blocks):
    moved = [blocks[0]]
    for e in range(1, Z_LO):
        moved.append(
            lax.ppermute(blocks[e], "seq", [(i, i ^ (e * YX)) for i in range(Z_LO * YX)])
        )
    return moved


def across_yx(blocks):
    groups = [[g * YX + t for t in range(YX)] for g in range(Z_LO)]
    return lax.all_to_all(
        jnp.stack(blocks, axis=1),
        "seq",
        split_axis=0,
        concat_axis=0,
        axis_index_groups=groups,
        tiled=True,
    )


def swap(block, bit):
    return lax.ppermute(block, "dp", [(i, i ^ bit) for i in range(4)])


def shards(
    inputs,
    grad_out,
    factor_one,
    factor_two,
    factor_three,
    factor_four,
    twiddle_in,
    twiddle_out,
    filter_freq,
    skip_gain,
):
    batch, chans, local_len = inputs.shape
    signal = inputs.reshape(chans, local_len)
    upstream = grad_out.reshape(chans, local_len)
    square = pltpu.VMEM((WIDTH, WIDTH), BF16)
    tall = pltpu.VMEM((WIDTH * ROWS, LANES), F32)

    sent = call(first_body, BLOCKS, [square, tall], signal, factor_one, twiddle_in)
    got = across_yx(across_z(sent))
    back = call(back_body, BLOCKS, [square, tall], upstream, factor_four)
    back_got = across_yx(across_z(back))

    filt = jnp.transpose(filter_freq, (1, 2, 0))
    spread, *mixed = call(
        middle_body,
        [struct((ROWS, WIDTH, LANES))] + BLOCKS,
        [square, square],
        got,
        factor_two.T,
        factor_three.T,
        twiddle_out,
        filt,
    )
    returned = across_yx(across_z(mixed))

    half = struct((ROWS, WIDTH // 2, LANES))
    keep, send = call(
        grad_body, [half, half], [square], back_got, factor_three, twiddle_out, spread
    )
    pair = call(add_body, half, [], keep, swap(send, 1))
    flat = struct((LANES * ROWS, WIDTH // 2))
    mine = call(
        total_body, flat, [pltpu.VMEM((LANES * ROWS, LANES), F32)], pair, swap(pair, 2)
    )
    filter_grad = call(join_body, struct((LANES * ROWS, WIDTH)), [], mine, swap(mine, 1))

    outputs = call(
        last_body,
        struct((chans, local_len)),
        [square, tall],
        returned,
        factor_four,
        signal,
        skip_gain.reshape(chans, 1),
    )
    return (
        outputs.reshape(batch, chans, local_len),
        filter_grad.reshape(chans, ROWS, WIDTH),
    )


def solution(mesh):
    in_specs = (
        P("dp", None, "seq"),
        P("dp", None, "seq"),
        P(),
        P(),
        P(),
        P(),
        P("seq", None),
        P("seq", None),
        P(None, "seq", None),
        P(),
    )
    out_specs = (P("dp", None, "seq"), P(None, "seq", None))
    return jax.shard_map(shards, mesh=mesh, in_specs=in_specs, out_specs=out_specs, check_vma=False)
```

```python
import jax
import jax.numpy as jnp
from jax import lax
from jax.experimental import pallas as pl
from jax.experimental.pallas import tpu as pltpu
from jax.sharding import PartitionSpec as P

F32 = jnp.float32
BF16 = jnp.bfloat16
LANES = 128
ROWS = 8
WIDTH = 512
HALF = WIDTH // 2
Z_LO = 4
YX = 16
PART = WIDTH // Z_LO
MSG = ROWS * ROWS
PAIRS = ROWS // 2
MIDDLE_US = 60
GRAD_US = 60

NT = (((1,), (1,)), ((), ()))
NN = (((1,), (0,)), ((), ()))
TN = (((0,), (0,)), ((), ()))


def dot(left, right, dims=NN):
    return lax.dot_general(left, right, dims, preferred_element_type=F32)


def my_z():
    return lax.axis_index("seq") // YX


def my_core():
    return lax.axis_index("dp") % 2


def part(z, e):
    return pl.ds(pl.multiple_of((z ^ e) * PART, PART), PART)


def halves(core):
    return pl.ds(pl.multiple_of(core * HALF, HALF), HALF)


def struct(shape, dtype=BF16):
    return jax.ShapeDtypeStruct(shape, dtype)


BLOCK = struct((YX, MSG, LANES))
WHOLE = struct((YX, Z_LO, MSG, LANES))
SQUARE = pltpu.VMEM((WIDTH, WIDTH), BF16)
TALL = pltpu.VMEM((WIDTH * ROWS, LANES), F32)


class Copies:
    def __init__(self, sems):
        self.sems = sems
        self.started = []
        self.waited = set()
        self.inputs = {}

    def start(self, src, dst):
        copy = pltpu.make_async_copy(src, dst, self.sems.at[len(self.started)])
        copy.start()
        self.started.append(copy)

    def fetch(self, arg, src, dst):
        self.inputs[arg] = len(self.started)
        self.start(src, dst)

    def wait(self, *args):
        for arg in args:
            self.finish(self.inputs.get(arg))

    def finish(self, n):
        if n is not None and n not in self.waited:
            self.waited.add(n)
            self.started[n].wait()

    def finish_all(self):
        for n in range(len(self.started)):
            self.finish(n)


class Far:
    def __init__(self, value, pinned=True):
        self.value = value
        self.pinned = pinned


def call(body, outs, scratch, *args, copies=0, weight_us=0):
    n_in, n_out = len(args), len(outs)
    far_in = [n for n, a in enumerate(args) if isinstance(a, Far)]
    far_out = [n for n, o in enumerate(outs) if isinstance(o, Far)]
    pinned = [n for n in far_in if args[n].pinned]
    args = [a.value if isinstance(a, Far) else a for a in args]
    outs = [o.value if isinstance(o, Far) else o for o in outs]
    hbm = pl.BlockSpec(memory_space=pltpu.HBM)
    free = pl.BlockSpec(memory_space=pl.ANY)
    vmem = pl.BlockSpec(memory_space=pltpu.VMEM)

    def space(n):
        return hbm if n in pinned else free if n in far_in else vmem

    def wrapped(*refs):
        refs = list(refs)
        ins, refs = refs[:n_in], refs[n_in:]
        results, refs = refs[:n_out], refs[n_out:]
        flow = Copies(refs.pop(0))
        for n in far_in:
            near = refs.pop(0)
            flow.fetch(n, ins[n], near)
            ins[n] = near
        near_results = list(results)
        for n in far_out:
            near_results[n] = refs.pop(0)
        body(flow, ins, results, near_results, *refs)
        flow.finish_all()

    return pl.pallas_call(
        wrapped,
        out_shape=[
            pltpu.HBM(o.shape, o.dtype) if n in far_out else o for n, o in enumerate(outs)
        ],
        in_specs=[space(n) for n in range(n_in)],
        out_specs=[hbm if n in far_out else vmem for n in range(n_out)],
        scratch_shapes=[pltpu.SemaphoreType.DMA((max(1, len(far_in) + copies),))]
        + [pltpu.VMEM(args[n].shape, args[n].dtype) for n in far_in]
        + [pltpu.VMEM(outs[n].shape, outs[n].dtype) for n in far_out]
        + scratch,
        compiler_params=pltpu.CompilerParams(vmem_limit_bytes=16 * 1024 * 1024),
        cost_estimate=pl.CostEstimate(
            flops=weight_us * 10**9, bytes_accessed=weight_us * 3 * 10**6, transcendentals=0
        ),
    )(
        *[
            pltpu.with_memory_space_constraint(a, pltpu.HBM) if n in pinned else a
            for n, a in enumerate(args)
        ]
    )


def rows_out(weight_scr, x_ref, twist, scr, finish):
    for pair in range(PAIRS):
        left = x_ref[:, (2 * pair) * WIDTH : (2 * pair + 1) * WIDTH]
        right = x_ref[:, (2 * pair + 1) * WIDTH : (2 * pair + 2) * WIDTH]
        both = dot(weight_scr[...], jnp.concatenate([left, right], axis=0), NT)
        for half in range(2):
            r = 2 * pair + half
            value = both[:, half * LANES : (half + 1) * LANES]
            if twist is not None:
                value = value * twist[:, r : r + 1]
            scr[pl.ds(r, WIDTH, stride=ROWS), :] = value
    step = WIDTH * ROWS // Z_LO
    for e in range(Z_LO):
        finish(e, scr[e * step : (e + 1) * step, :].astype(BF16).reshape(YX, MSG, LANES))


def first_body(flow, ins, results, outs, fscr, scr):
    f_ref, tw_ref, x_ref = ins
    z = my_z()
    flow.wait(0, 1)
    twist = []
    for e in range(Z_LO):
        fscr[e * PART : (e + 1) * PART, :] = f_ref[:, part(z, e)].T
        twist.append(tw_ref[:, part(z, e)].astype(F32).T)
    flow.wait(2)

    def finish(e, block):
        outs[0][:, e] = block
        flow.start(outs[0].at[:, e], results[0].at[:, e])

    rows_out(fscr, x_ref, jnp.concatenate(twist, axis=0), scr, finish)


def back_body(flow, ins, results, outs, fscr, scr):
    f_ref, x_ref = ins
    z = my_z()
    flow.wait(0)
    for e in range(Z_LO):
        fscr[e * PART : (e + 1) * PART, :] = f_ref[part(z, e), :]
    flow.wait(1)

    def finish(e, block):
        outs[e][...] = block

    rows_out(fscr, x_ref, None, scr, finish)


def columns(refs, pair):
    got = [[], []]
    for ref in refs:
        block = ref[:, pair * 16 : (pair + 1) * 16, :].astype(F32)
        block = block.reshape(YX, 2, ROWS, LANES)
        for half in range(2):
            got[half].append(block[:, half].reshape(PART, LANES))
    return [jnp.concatenate(parts, axis=0) for parts in got]


def twist_columns(tw_ref, z):
    return jnp.concatenate(
        [tw_ref[:, part(z, e)].astype(F32).T for e in range(Z_LO)], axis=0
    )


def middle_body(flow, ins, results, outs, f2s, f3s):
    f2t_ref, tw_ref, u0, u1, u2, u3, filt_ref, f3t_ref = ins
    zt_ref, *blocks = outs
    z = my_z()
    flow.wait(0, 1)
    for e in range(Z_LO):
        f2s[:, e * PART : (e + 1) * PART] = f2t_ref[:, part(z, e)]
    twist = twist_columns(tw_ref, z)
    for pair in range(PAIRS):
        k = 2 * pair
        cols = columns((u0, u1, u2, u3), pair)
        rhs = jnp.concatenate([c.astype(BF16) for c in cols], axis=1)
        spread = dot(f2s[...], rhs).astype(BF16)
        zt_ref[k] = spread[:, :LANES]
        zt_ref[k + 1] = spread[:, LANES:]
        if pair == 0:
            flow.wait(6, 7)
            for e in range(Z_LO):
                f3s[e * PART : (e + 1) * PART, :] = f3t_ref[part(z, e), :]
        filt = jnp.concatenate([filt_ref[k], filt_ref[k + 1]], axis=1)
        filtered = (spread.astype(F32) * filt.astype(F32)).astype(BF16)
        third = dot(f3s[...], filtered)
        first = third[:, :LANES] * twist[:, k : k + 1]
        second = third[:, LANES:] * twist[:, k + 1 : k + 2]
        shaped = jnp.concatenate(
            [first.reshape(Z_LO * YX, ROWS, LANES), second.reshape(Z_LO * YX, ROWS, LANES)],
            axis=1,
        ).astype(BF16)
        rows = slice(pair * 16, (pair + 1) * 16)
        for e, block in enumerate(blocks):
            block[:, rows, :] = shaped[e * YX : (e + 1) * YX]
        flow.start(zt_ref.at[k : k + 2], results[0].at[k : k + 2])


def grad_body(flow, ins, results, outs, f3s):
    f3_ref, tw_ref, d_ref, zt_ref = ins
    z = my_z()
    core = my_core()
    spans = (halves(core), halves(1 - core))
    flow.wait(0, 1)
    for n, span in enumerate(spans):
        for e in range(Z_LO):
            f3s[n * HALF : (n + 1) * HALF, e * PART : (e + 1) * PART] = f3_ref[span, part(z, e)]
    twist = twist_columns(tw_ref, z)
    for pair in range(PAIRS):
        k = 2 * pair
        cols = columns([d_ref.at[:, e] for e in range(Z_LO)], pair)
        rhs = jnp.concatenate(
            [(cols[h] * twist[:, k + h : k + h + 1]).astype(BF16) for h in range(2)], axis=1
        )
        grads = dot(f3s[...], rhs)
        flow.wait(3)
        for h in range(2):
            value = grads[:, h * LANES : (h + 1) * LANES]
            for n, (span, out) in enumerate(zip(spans, outs)):
                spread = zt_ref[k + h, span, :].astype(F32)
                out[k + h] = (spread * value[n * HALF : (n + 1) * HALF]).astype(BF16)


def last_body(flow, ins, results, outs, fscr, scr):
    f_ref, g_ref, s_ref, x_ref = ins
    o_ref = outs[0]
    z = my_z()
    step = YX * MSG
    flow.wait(0)
    for e in range(Z_LO):
        fscr[e * PART : (e + 1) * PART, :] = f_ref[part(z, e), :]
        scr[e * step : (e + 1) * step, :] = s_ref[:, e].astype(F32).reshape(step, LANES)
    flow.wait(1, 3)
    gains = g_ref[...]
    for r in range(ROWS):
        rows = scr[pl.ds(r, WIDTH, stride=ROWS), :].astype(BF16)
        fourth = dot(rows, fscr[...], TN)
        span = slice(r * WIDTH, (r + 1) * WIDTH)
        signal = x_ref[:, span].astype(F32)
        o_ref[:, span] = (fourth + gains * signal).astype(BF16)
        flow.start(o_ref.at[:, span], results[0].at[:, span])


def add_body(flow, ins, results, outs):
    outs[0][...] = (ins[0][...].astype(F32) + ins[1][...].astype(F32)).astype(BF16)


def total_body(flow, ins, results, outs, scr):
    a_ref, b_ref = ins
    for side in range(2):
        span = slice(side * LANES, (side + 1) * LANES)
        for k in range(ROWS):
            total = a_ref[k, span, :].astype(F32) + b_ref[k, span, :].astype(F32)
            scr[pl.ds(k, LANES, stride=ROWS), :] = total.T
        outs[0][:, span] = scr[...].astype(BF16)


def join_body(flow, ins, results, outs):
    core = my_core()
    outs[0][:, halves(core)] = ins[0][...]
    outs[0][:, halves(1 - core)] = ins[1][...]
    flow.start(outs[0], results[0])


def gather_body(flow, ins, results, outs):
    for e, block in enumerate(ins):
        outs[0][:, e] = block[...]
        flow.start(outs[0].at[:, e], results[0].at[:, e])


def spread_body(flow, ins, results, outs):
    for e, block in enumerate(outs):
        block[...] = ins[0][:, e]


def gathered(blocks):
    return call(gather_body, [Far(WHOLE)], [], *blocks, copies=Z_LO)[0]


def scattered(whole):
    return call(spread_body, [BLOCK] * Z_LO, [], whole)


def across_z(blocks):
    moved = [blocks[0]]
    for e in range(1, Z_LO):
        moved.append(
            lax.ppermute(blocks[e], "seq", [(i, i ^ (e * YX)) for i in range(Z_LO * YX)])
        )
    return moved


def tied(*values):
    return lax.optimization_barrier(values)


def across_yx(whole):
    groups = [[g * YX + t for t in range(YX)] for g in range(Z_LO)]
    return lax.all_to_all(
        whole, "seq", split_axis=0, concat_axis=0, axis_index_groups=groups, tiled=True
    )


def swap(block, bit):
    return lax.ppermute(block, "dp", [(i, i ^ bit) for i in range(4)])


def shards(
    inputs,
    grad_out,
    factor_one,
    factor_two,
    factor_three,
    factor_four,
    twiddle_in,
    twiddle_out,
    filter_freq,
    skip_gain,
):
    batch, chans, local_len = inputs.shape
    signal = inputs.reshape(chans, local_len)
    upstream = grad_out.reshape(chans, local_len)

    sent = call(
        first_body,
        [Far(WHOLE)],
        [SQUARE, TALL],
        Far(factor_one),
        Far(twiddle_in),
        Far(signal),
        copies=Z_LO,
    )[0]
    back = call(back_body, [BLOCK] * Z_LO, [SQUARE, TALL], Far(factor_four), Far(upstream))
    filt = jnp.transpose(filter_freq, (1, 2, 0))
    gains = skip_gain.reshape(chans, 1)
    moved, filt, two, three, gains = tied(
        across_yx(sent), filt, factor_two.T, factor_three.T, gains
    )
    got = across_z(scattered(moved))
    back_got = across_yx(gathered(across_z(back)))

    spread, *mixed = call(
        middle_body,
        [Far(struct((ROWS, WIDTH, LANES)))] + [BLOCK] * Z_LO,
        [SQUARE, SQUARE],
        Far(two),
        Far(twiddle_out),
        *got,
        Far(filt),
        Far(three),
        copies=PAIRS,
        weight_us=MIDDLE_US,
    )
    half = struct((ROWS, HALF, LANES))
    keep, send = call(
        grad_body,
        [half, half],
        [SQUARE],
        Far(factor_three),
        Far(twiddle_out),
        back_got,
        Far(spread),
        weight_us=GRAD_US,
    )
    mixed_arrived, keep, send = tied(across_z(mixed), keep, send)
    pair = call(add_body, [half], [], keep, swap(send, 1))[0]
    far = swap(pair, 2)
    returned = across_yx(gathered(mixed_arrived))
    flat = struct((LANES * ROWS, HALF))
    mine = call(total_body, [flat], [pltpu.VMEM((LANES * ROWS, LANES), F32)], pair, far)[0]
    filter_grad = call(
        join_body, [Far(struct((LANES * ROWS, WIDTH)))], [], mine, swap(mine, 1), copies=1
    )[0]

    outputs = call(
        last_body,
        [Far(struct((chans, local_len)))],
        [SQUARE, TALL],
        Far(factor_four),
        Far(gains),
        returned,
        Far(signal),
        copies=ROWS,
    )[0]
    return (
        outputs.reshape(batch, chans, local_len),
        filter_grad.reshape(chans, ROWS, WIDTH),
    )


def solution(mesh):
    in_specs = (
        P("dp", None, "seq"),
        P("dp", None, "seq"),
        P(),
        P(),
        P(),
        P(),
        P("seq", None),
        P("seq", None),
        P(None, "seq", None),
        P(),
    )
    out_specs = (P("dp", None, "seq"), P(None, "seq", None))
    return jax.shard_map(shards, mesh=mesh, in_specs=in_specs, out_specs=out_specs, check_vma=False)
```

```python
import jax
import jax.numpy as jnp
from jax import lax
from jax.experimental import pallas as pl
from jax.experimental.pallas import tpu as pltpu
from jax.sharding import PartitionSpec as P

F32 = jnp.float32
BF16 = jnp.bfloat16
LANES = 128
ROWS = 8
WIDTH = 512
HALF = WIDTH // 2
Z_LO = 4
YX = 16
PART = WIDTH // Z_LO
MSG = ROWS * ROWS
PAIRS = ROWS // 2
EXCHANGE_US = 60

NT = (((1,), (1,)), ((), ()))
NN = (((1,), (0,)), ((), ()))
TN = (((0,), (0,)), ((), ()))


def dot(left, right, dims=NN):
    return lax.dot_general(left, right, dims, preferred_element_type=F32)


def my_z():
    return lax.axis_index("seq") // YX


def my_core():
    return lax.axis_index("dp") % 2


def part(z, e):
    return pl.ds(pl.multiple_of((z ^ e) * PART, PART), PART)


def halves(core):
    return pl.ds(pl.multiple_of(core * HALF, HALF), HALF)


def struct(shape, dtype=BF16):
    return jax.ShapeDtypeStruct(shape, dtype)


BLOCK = struct((YX, MSG, LANES))
WHOLE = struct((YX, Z_LO, MSG, LANES))
SQUARE = pltpu.VMEM((WIDTH, WIDTH), BF16)
TALL = pltpu.VMEM((WIDTH * ROWS, LANES), F32)


class Copies:
    def __init__(self, sems):
        self.sems = sems
        self.started = []
        self.waited = set()
        self.inputs = {}

    def start(self, src, dst):
        copy = pltpu.make_async_copy(src, dst, self.sems.at[len(self.started)])
        copy.start()
        self.started.append(copy)

    def fetch(self, arg, src, dst):
        self.inputs[arg] = len(self.started)
        self.start(src, dst)

    def wait(self, *args):
        for arg in args:
            self.finish(self.inputs.get(arg))

    def finish(self, n):
        if n is not None and n not in self.waited:
            self.waited.add(n)
            self.started[n].wait()

    def finish_all(self):
        for n in range(len(self.started)):
            self.finish(n)


class Far:
    def __init__(self, value, pinned=True):
        self.value = value
        self.pinned = pinned


def call(body, outs, scratch, *args, copies=0, weight_us=0):
    n_in, n_out = len(args), len(outs)
    far_in = [n for n, a in enumerate(args) if isinstance(a, Far)]
    far_out = [n for n, o in enumerate(outs) if isinstance(o, Far)]
    pinned = [n for n in far_in if args[n].pinned]
    args = [a.value if isinstance(a, Far) else a for a in args]
    outs = [o.value if isinstance(o, Far) else o for o in outs]
    hbm = pl.BlockSpec(memory_space=pltpu.HBM)
    free = pl.BlockSpec(memory_space=pl.ANY)
    vmem = pl.BlockSpec(memory_space=pltpu.VMEM)

    def space(n):
        return hbm if n in pinned else free if n in far_in else vmem

    def wrapped(*refs):
        refs = list(refs)
        ins, refs = refs[:n_in], refs[n_in:]
        results, refs = refs[:n_out], refs[n_out:]
        flow = Copies(refs.pop(0))
        for n in far_in:
            near = refs.pop(0)
            flow.fetch(n, ins[n], near)
            ins[n] = near
        near_results = list(results)
        for n in far_out:
            near_results[n] = refs.pop(0)
        body(flow, ins, results, near_results, *refs)
        flow.finish_all()

    return pl.pallas_call(
        wrapped,
        out_shape=[
            pltpu.HBM(o.shape, o.dtype) if n in far_out else o for n, o in enumerate(outs)
        ],
        in_specs=[space(n) for n in range(n_in)],
        out_specs=[hbm if n in far_out else vmem for n in range(n_out)],
        scratch_shapes=[pltpu.SemaphoreType.DMA((max(1, len(far_in) + copies),))]
        + [pltpu.VMEM(args[n].shape, args[n].dtype) for n in far_in]
        + [pltpu.VMEM(outs[n].shape, outs[n].dtype) for n in far_out]
        + scratch,
        compiler_params=pltpu.CompilerParams(vmem_limit_bytes=16 * 1024 * 1024),
        cost_estimate=pl.CostEstimate(
            flops=weight_us * 10**9, bytes_accessed=weight_us * 3 * 10**6, transcendentals=0
        ),
    )(
        *[
            pltpu.with_memory_space_constraint(a, pltpu.HBM) if n in pinned else a
            for n, a in enumerate(args)
        ]
    )


def rows_out(weight_scr, x_ref, twist, scr, finish):
    for pair in range(PAIRS):
        left = x_ref[:, (2 * pair) * WIDTH : (2 * pair + 1) * WIDTH]
        right = x_ref[:, (2 * pair + 1) * WIDTH : (2 * pair + 2) * WIDTH]
        both = dot(weight_scr[...], jnp.concatenate([left, right], axis=0), NT)
        for half in range(2):
            r = 2 * pair + half
            value = both[:, half * LANES : (half + 1) * LANES]
            if twist is not None:
                value = value * twist[:, r : r + 1]
            scr[pl.ds(r, WIDTH, stride=ROWS), :] = value
    step = WIDTH * ROWS // Z_LO
    for e in range(Z_LO):
        finish(e, scr[e * step : (e + 1) * step, :].astype(BF16).reshape(YX, MSG, LANES))


def first_body(flow, ins, results, outs, fscr, scr):
    f_ref, tw_ref, x_ref = ins
    z = my_z()
    flow.wait(0, 1)
    twist = []
    for e in range(Z_LO):
        fscr[e * PART : (e + 1) * PART, :] = f_ref[:, part(z, e)].T
        twist.append(tw_ref[:, part(z, e)].astype(F32).T)
    flow.wait(2)

    def finish(e, block):
        outs[0][:, e] = block
        flow.start(outs[0].at[:, e], results[0].at[:, e])

    rows_out(fscr, x_ref, jnp.concatenate(twist, axis=0), scr, finish)


def back_body(flow, ins, results, outs, fscr, scr):
    f_ref, x_ref = ins
    z = my_z()
    flow.wait(0)
    for e in range(Z_LO):
        fscr[e * PART : (e + 1) * PART, :] = f_ref[part(z, e), :]
    flow.wait(1)

    def finish(e, block):
        outs[e][...] = block

    rows_out(fscr, x_ref, None, scr, finish)


def columns(refs, pair):
    got = [[], []]
    for ref in refs:
        block = ref[:, pair * 16 : (pair + 1) * 16, :].astype(F32)
        block = block.reshape(YX, 2, ROWS, LANES)
        for half in range(2):
            got[half].append(block[:, half].reshape(PART, LANES))
    return [jnp.concatenate(parts, axis=0) for parts in got]


def twist_columns(tw_ref, z):
    return jnp.concatenate(
        [tw_ref[:, part(z, e)].astype(F32).T for e in range(Z_LO)], axis=0
    )


def middle_body(flow, ins, results, outs, f2s, f3s):
    f2t_ref, tw_ref, u0, u1, u2, u3, filt_ref, f3t_ref = ins
    zt_ref, *blocks = outs
    z = my_z()
    flow.wait(0, 1)
    for e in range(Z_LO):
        f2s[:, e * PART : (e + 1) * PART] = f2t_ref[:, part(z, e)]
    twist = twist_columns(tw_ref, z)
    for pair in range(PAIRS):
        k = 2 * pair
        cols = columns((u0, u1, u2, u3), pair)
        rhs = jnp.concatenate([c.astype(BF16) for c in cols], axis=1)
        spread = dot(f2s[...], rhs).astype(BF16)
        zt_ref[k] = spread[:, :LANES]
        zt_ref[k + 1] = spread[:, LANES:]
        if pair == 0:
            flow.wait(6, 7)
            for e in range(Z_LO):
                f3s[e * PART : (e + 1) * PART, :] = f3t_ref[part(z, e), :]
        filt = jnp.concatenate([filt_ref[k], filt_ref[k + 1]], axis=1)
        filtered = (spread.astype(F32) * filt.astype(F32)).astype(BF16)
        third = dot(f3s[...], filtered)
        first = third[:, :LANES] * twist[:, k : k + 1]
        second = third[:, LANES:] * twist[:, k + 1 : k + 2]
        shaped = jnp.concatenate(
            [first.reshape(Z_LO * YX, ROWS, LANES), second.reshape(Z_LO * YX, ROWS, LANES)],
            axis=1,
        ).astype(BF16)
        rows = slice(pair * 16, (pair + 1) * 16)
        for e, block in enumerate(blocks):
            block[:, rows, :] = shaped[e * YX : (e + 1) * YX]
        flow.start(zt_ref.at[k : k + 2], results[0].at[k : k + 2])


def grad_body(flow, ins, results, outs, f3s):
    f3_ref, tw_ref, d_ref, zt_ref = ins
    z = my_z()
    core = my_core()
    spans = (halves(core), halves(1 - core))
    flow.wait(0, 1)
    for n, span in enumerate(spans):
        for e in range(Z_LO):
            f3s[n * HALF : (n + 1) * HALF, e * PART : (e + 1) * PART] = f3_ref[span, part(z, e)]
    twist = twist_columns(tw_ref, z)
    for pair in range(PAIRS):
        k = 2 * pair
        cols = columns([d_ref.at[:, e] for e in range(Z_LO)], pair)
        rhs = jnp.concatenate(
            [(cols[h] * twist[:, k + h : k + h + 1]).astype(BF16) for h in range(2)], axis=1
        )
        grads = dot(f3s[...], rhs)
        flow.wait(3)
        for h in range(2):
            value = grads[:, h * LANES : (h + 1) * LANES]
            for n, (span, out) in enumerate(zip(spans, outs)):
                spread = zt_ref[k + h, span, :].astype(F32)
                out[k + h] = (spread * value[n * HALF : (n + 1) * HALF]).astype(BF16)


def last_body(flow, ins, results, outs, fscr, scr):
    f_ref, g_ref, s_ref, x_ref = ins
    o_ref = outs[0]
    z = my_z()
    step = YX * MSG
    for e in range(Z_LO):
        scr[e * step : (e + 1) * step, :] = s_ref[:, e].astype(F32).reshape(step, LANES)
    flow.wait(0)
    for e in range(Z_LO):
        fscr[e * PART : (e + 1) * PART, :] = f_ref[part(z, e), :]
    flow.wait(1, 3)
    gains = g_ref[...]
    for r in range(ROWS):
        rows = scr[pl.ds(r, WIDTH, stride=ROWS), :].astype(BF16)
        fourth = dot(rows, fscr[...], TN)
        span = slice(r * WIDTH, (r + 1) * WIDTH)
        signal = x_ref[:, span].astype(F32)
        o_ref[:, span] = (fourth + gains * signal).astype(BF16)
        flow.start(o_ref.at[:, span], results[0].at[:, span])


def add_body(flow, ins, results, outs):
    for n, out in enumerate(outs):
        span = slice(n * LANES, (n + 1) * LANES)
        out[...] = (ins[0][:, span].astype(F32) + ins[1][:, span].astype(F32)).astype(BF16)


def total_body(flow, ins, results, outs, scr):
    a_ref, b_ref = ins
    for k in range(ROWS):
        total = a_ref[k].astype(F32) + b_ref[k].astype(F32)
        scr[pl.ds(k, LANES, stride=ROWS), :] = total.T
    outs[0][...] = scr[...].astype(BF16)


def join_body(flow, ins, results, outs):
    core = my_core()
    for n, block in enumerate(ins):
        owner = core if n < 2 else 1 - core
        place = pl.multiple_of(owner * HALF + (n % 2) * LANES, LANES)
        outs[0][:, pl.ds(place, LANES)] = block[...]
    flow.start(outs[0], results[0])


def gather_body(flow, ins, results, outs):
    for e, block in enumerate(ins):
        flow.start(block, results[0].at[:, e])


def spread_body(flow, ins, results, outs):
    for e, block in enumerate(outs):
        block[...] = ins[0][:, e]


def gathered(blocks):
    return call(
        gather_body, [Far(WHOLE)], [], *blocks, copies=Z_LO, weight_us=EXCHANGE_US
    )[0]


def scattered(whole):
    return call(spread_body, [BLOCK] * Z_LO, [], whole)


def across_z(blocks):
    moved = [blocks[0]]
    for e in range(1, Z_LO):
        moved.append(
            lax.ppermute(blocks[e], "seq", [(i, i ^ (e * YX)) for i in range(Z_LO * YX)])
        )
    return moved


def tied(*values):
    return lax.optimization_barrier(values)


def across_yx(whole):
    groups = [[g * YX + t for t in range(YX)] for g in range(Z_LO)]
    return lax.all_to_all(
        whole, "seq", split_axis=0, concat_axis=0, axis_index_groups=groups, tiled=True
    )


def swap(block, bit):
    return lax.ppermute(block, "dp", [(i, i ^ bit) for i in range(4)])


def shards(
    inputs,
    grad_out,
    factor_one,
    factor_two,
    factor_three,
    factor_four,
    twiddle_in,
    twiddle_out,
    filter_freq,
    skip_gain,
):
    batch, chans, local_len = inputs.shape
    signal = inputs.reshape(chans, local_len)
    upstream = grad_out.reshape(chans, local_len)

    sent = call(
        first_body,
        [Far(WHOLE)],
        [SQUARE, TALL],
        factor_one,
        twiddle_in,
        signal,
        copies=Z_LO,
        weight_us=EXCHANGE_US,
    )[0]
    back = call(back_body, [BLOCK] * Z_LO, [SQUARE, TALL], Far(factor_four), Far(upstream))
    filt = jnp.transpose(filter_freq, (1, 2, 0))
    gains = skip_gain.reshape(chans, 1)
    moved, back_whole, filt, two, three, gains = tied(
        across_yx(sent),
        gathered(across_z(back)),
        filt,
        factor_two.T,
        factor_three.T,
        gains,
    )
    got = across_z(scattered(moved))
    back_got = across_yx(back_whole)

    spread, *mixed = call(
        middle_body,
        [Far(struct((ROWS, WIDTH, LANES)))] + [BLOCK] * Z_LO,
        [SQUARE, SQUARE],
        Far(two),
        Far(twiddle_out),
        *got,
        Far(filt),
        Far(three),
        copies=PAIRS,
        weight_us=EXCHANGE_US,
    )
    half = struct((ROWS, HALF, LANES))
    keep, send = call(
        grad_body,
        [half, half],
        [SQUARE],
        Far(factor_three),
        Far(twiddle_out),
        back_got,
        Far(spread),
        weight_us=EXCHANGE_US,
    )
    mixed_whole = gathered(across_z(mixed))
    quarter = struct((ROWS, LANES, LANES))
    pairs = call(add_body, [quarter] * 2, [], keep, swap(send, 1))
    mixed_whole, pairs = tied(mixed_whole, pairs)
    returned = across_yx(mixed_whole)
    flat = struct((LANES * ROWS, LANES))
    far = [swap(pair, 2) for pair in pairs]
    outputs = call(
        last_body,
        [Far(struct((chans, local_len)))],
        [SQUARE, TALL],
        factor_four,
        gains,
        returned,
        signal,
        copies=ROWS,
    )[0]
    far[1], outputs = tied(far[1], outputs)
    mine = [
        call(total_body, [flat], [pltpu.VMEM(flat.shape, F32)], pair, got_far, weight_us=weight)[0]
        for pair, got_far, weight in zip(pairs, far, (0, 0))
    ]
    other = [swap(total, 1) for total in mine]
    filter_grad = call(
        join_body, [Far(struct((LANES * ROWS, WIDTH)))], [], *mine, *other, copies=1
    )[0]

    return (
        outputs.reshape(batch, chans, local_len),
        filter_grad.reshape(chans, ROWS, WIDTH),
    )


def solution(mesh):
    in_specs = (
        P("dp", None, "seq"),
        P("dp", None, "seq"),
        P(),
        P(),
        P(),
        P(),
        P("seq", None),
        P("seq", None),
        P(None, "seq", None),
        P(),
    )
    out_specs = (P("dp", None, "seq"), P(None, "seq", None))
    return jax.shard_map(shards, mesh=mesh, in_specs=in_specs, out_specs=out_specs, check_vma=False)
```

```python
import jax
import jax.numpy as jnp
from jax import lax
from jax.experimental import pallas as pl
from jax.experimental.pallas import tpu as pltpu
from jax.sharding import PartitionSpec as P

F32 = jnp.float32
BF16 = jnp.bfloat16
LANES = 128
ROWS = 8
WIDTH = 512
HALF = WIDTH // 2
Z_LO = 4
YX = 16
PART = WIDTH // Z_LO
MSG = ROWS * ROWS
PAIRS = ROWS // 2
EXCHANGE_US = 60

NT = (((1,), (1,)), ((), ()))
NN = (((1,), (0,)), ((), ()))
TN = (((0,), (0,)), ((), ()))


def dot(left, right, dims=NN):
    return lax.dot_general(left, right, dims, preferred_element_type=F32)


def my_z():
    return lax.axis_index("seq") // YX


def my_core():
    return lax.axis_index("dp") % 2


def part(z, e):
    return pl.ds(pl.multiple_of((z ^ e) * PART, PART), PART)


def halves(core):
    return pl.ds(pl.multiple_of(core * HALF, HALF), HALF)


def struct(shape, dtype=BF16):
    return jax.ShapeDtypeStruct(shape, dtype)


BLOCK = struct((YX, MSG, LANES))
WHOLE = struct((YX, Z_LO, MSG, LANES))
SQUARE = pltpu.VMEM((WIDTH, WIDTH), BF16)
TALL = pltpu.VMEM((WIDTH * ROWS, LANES), F32)


class Copies:
    def __init__(self, sems):
        self.sems = sems
        self.started = []
        self.waited = set()
        self.inputs = {}

    def start(self, src, dst):
        copy = pltpu.make_async_copy(src, dst, self.sems.at[len(self.started)])
        copy.start()
        self.started.append(copy)

    def fetch(self, arg, src, dst):
        self.inputs[arg] = len(self.started)
        self.start(src, dst)

    def wait(self, *args):
        for arg in args:
            self.finish(self.inputs.get(arg))

    def finish(self, n):
        if n is not None and n not in self.waited:
            self.waited.add(n)
            self.started[n].wait()

    def finish_all(self):
        for n in range(len(self.started)):
            self.finish(n)


class Far:
    def __init__(self, value, pinned=True):
        self.value = value
        self.pinned = pinned


def call(body, outs, scratch, *args, copies=0, weight_us=0, fetch=None, aliases=None):
    n_in, n_out = len(args), len(outs)
    far_in = [n for n, a in enumerate(args) if isinstance(a, Far)]
    far_out = [n for n, o in enumerate(outs) if isinstance(o, Far)]
    pinned = [n for n in far_in if args[n].pinned]
    args = [a.value if isinstance(a, Far) else a for a in args]
    outs = [o.value if isinstance(o, Far) else o for o in outs]
    hbm = pl.BlockSpec(memory_space=pltpu.HBM)
    free = pl.BlockSpec(memory_space=pl.ANY)
    vmem = pl.BlockSpec(memory_space=pltpu.VMEM)

    def space(n):
        return hbm if n in pinned else free if n in far_in else vmem

    fetched = [n for n in far_in if fetch is None or n in fetch]

    def wrapped(*refs):
        refs = list(refs)
        ins, refs = refs[:n_in], refs[n_in:]
        results, refs = refs[:n_out], refs[n_out:]
        flow = Copies(refs.pop(0))
        for n in fetched:
            near = refs.pop(0)
            flow.fetch(n, ins[n], near)
            ins[n] = near
        near_results = list(results)
        for n in far_out:
            near_results[n] = refs.pop(0)
        body(flow, ins, results, near_results, *refs)
        flow.finish_all()

    return pl.pallas_call(
        wrapped,
        out_shape=[
            pltpu.HBM(o.shape, o.dtype) if n in far_out else o for n, o in enumerate(outs)
        ],
        in_specs=[space(n) for n in range(n_in)],
        out_specs=[hbm if n in far_out else vmem for n in range(n_out)],
        scratch_shapes=[pltpu.SemaphoreType.DMA((max(1, len(far_in) + copies),))]
        + [pltpu.VMEM(args[n].shape, args[n].dtype) for n in fetched]
        + [pltpu.VMEM(outs[n].shape, outs[n].dtype) for n in far_out]
        + scratch,
        input_output_aliases=aliases or {},
        compiler_params=pltpu.CompilerParams(vmem_limit_bytes=16 * 1024 * 1024),
        cost_estimate=pl.CostEstimate(
            flops=weight_us * 10**9, bytes_accessed=weight_us * 3 * 10**6, transcendentals=0
        ),
    )(
        *[
            pltpu.with_memory_space_constraint(a, pltpu.HBM) if n in pinned else a
            for n, a in enumerate(args)
        ]
    )


def rows_out(weight_scr, x_ref, twist, scr, finish):
    for pair in range(PAIRS):
        left = x_ref[:, (2 * pair) * WIDTH : (2 * pair + 1) * WIDTH]
        right = x_ref[:, (2 * pair + 1) * WIDTH : (2 * pair + 2) * WIDTH]
        both = dot(weight_scr[...], jnp.concatenate([left, right], axis=0), NT)
        for half in range(2):
            r = 2 * pair + half
            value = both[:, half * LANES : (half + 1) * LANES]
            if twist is not None:
                value = value * twist[:, r : r + 1]
            scr[pl.ds(r, WIDTH, stride=ROWS), :] = value
    step = WIDTH * ROWS // Z_LO
    for e in range(Z_LO):
        finish(e, scr[e * step : (e + 1) * step, :].astype(BF16).reshape(YX, MSG, LANES))


def first_body(flow, ins, results, outs, fscr, scr):
    f_ref, tw_ref, x_ref = ins
    z = my_z()
    flow.wait(0, 1)
    twist = []
    for e in range(Z_LO):
        fscr[e * PART : (e + 1) * PART, :] = f_ref[:, part(z, e)].T
        twist.append(tw_ref[:, part(z, e)].astype(F32).T)
    flow.wait(2)

    def finish(e, block):
        outs[0][:, e] = block
        flow.start(outs[0].at[:, e], results[0].at[:, e])

    rows_out(fscr, x_ref, jnp.concatenate(twist, axis=0), scr, finish)


def back_body(flow, ins, results, outs, fscr, scr):
    f_ref, x_ref = ins
    z = my_z()
    flow.wait(0)
    for e in range(Z_LO):
        fscr[e * PART : (e + 1) * PART, :] = f_ref[part(z, e), :]
    flow.wait(1)

    def finish(e, block):
        outs[e][...] = block

    rows_out(fscr, x_ref, None, scr, finish)


def columns(refs, pair):
    got = [[], []]
    for ref in refs:
        block = ref[:, pair * 16 : (pair + 1) * 16, :].astype(F32)
        block = block.reshape(YX, 2, ROWS, LANES)
        for half in range(2):
            got[half].append(block[:, half].reshape(PART, LANES))
    return [jnp.concatenate(parts, axis=0) for parts in got]


def twist_columns(tw_ref, z):
    return jnp.concatenate(
        [tw_ref[:, part(z, e)].astype(F32).T for e in range(Z_LO)], axis=0
    )


def middle_body(flow, ins, results, outs, f2s, f3s, cols_scr, mid_scr):
    f2t_ref, tw_ref, u0, u1, u2, u3, filt_ref, f3t_ref = ins
    zt_ref, *blocks = outs
    z = my_z()
    for pair in range(PAIRS):
        cols = columns((u0, u1, u2, u3), pair)
        for half in range(2):
            span = slice(half * LANES, (half + 1) * LANES)
            cols_scr[pair, :, span] = cols[half].astype(BF16)
    flow.wait(0)
    for e in range(Z_LO):
        f2s[:, e * PART : (e + 1) * PART] = f2t_ref[:, part(z, e)]
    for pair in range(PAIRS):
        k = 2 * pair
        spread = dot(f2s[...], cols_scr[pair]).astype(BF16)
        zt_ref[k] = spread[:, :LANES]
        zt_ref[k + 1] = spread[:, LANES:]
        flow.start(zt_ref.at[k : k + 2], results[0].at[k : k + 2])
        flow.wait(6)
        filt = jnp.concatenate([filt_ref[k], filt_ref[k + 1]], axis=1)
        mid_scr[pair] = (spread.astype(F32) * filt.astype(F32)).astype(BF16)
    flow.wait(1, 7)
    twist = twist_columns(tw_ref, z)
    for e in range(Z_LO):
        f3s[e * PART : (e + 1) * PART, :] = f3t_ref[part(z, e), :]
    for pair in range(PAIRS):
        k = 2 * pair
        third = dot(f3s[...], mid_scr[pair])
        first = third[:, :LANES] * twist[:, k : k + 1]
        second = third[:, LANES:] * twist[:, k + 1 : k + 2]
        shaped = jnp.concatenate(
            [first.reshape(Z_LO * YX, ROWS, LANES), second.reshape(Z_LO * YX, ROWS, LANES)],
            axis=1,
        ).astype(BF16)
        rows = slice(pair * 16, (pair + 1) * 16)
        for e, block in enumerate(blocks):
            block[:, rows, :] = shaped[e * YX : (e + 1) * YX]


def grad_body(flow, ins, results, outs, f3s):
    f3_ref, tw_ref, d_ref, zt_ref = ins
    z = my_z()
    core = my_core()
    spans = (halves(core), halves(1 - core))
    flow.wait(0, 1)
    for n, span in enumerate(spans):
        for e in range(Z_LO):
            f3s[n * HALF : (n + 1) * HALF, e * PART : (e + 1) * PART] = f3_ref[span, part(z, e)]
    twist = twist_columns(tw_ref, z)
    for pair in range(PAIRS):
        k = 2 * pair
        cols = columns([d_ref.at[:, e] for e in range(Z_LO)], pair)
        rhs = jnp.concatenate(
            [(cols[h] * twist[:, k + h : k + h + 1]).astype(BF16) for h in range(2)], axis=1
        )
        grads = dot(f3s[...], rhs)
        flow.wait(3)
        for h in range(2):
            value = grads[:, h * LANES : (h + 1) * LANES]
            for n, (span, out) in enumerate(zip(spans, outs)):
                spread = zt_ref[k + h, span, :].astype(F32)
                out[k + h] = (spread * value[n * HALF : (n + 1) * HALF]).astype(BF16)


def last_body(flow, ins, results, outs, fscr, scr):
    f_ref, g_ref, s_ref, x_ref = ins
    o_ref = outs[0]
    z = my_z()
    step = YX * MSG
    for e in range(Z_LO):
        scr[e * step : (e + 1) * step, :] = s_ref[:, e].astype(F32).reshape(step, LANES)
    flow.wait(0)
    for e in range(Z_LO):
        fscr[e * PART : (e + 1) * PART, :] = f_ref[part(z, e), :]
    flow.wait(1, 3)
    gains = g_ref[...]
    for r in range(ROWS):
        rows = scr[pl.ds(r, WIDTH, stride=ROWS), :].astype(BF16)
        fourth = dot(rows, fscr[...], TN)
        span = slice(r * WIDTH, (r + 1) * WIDTH)
        signal = x_ref[:, span].astype(F32)
        o_ref[:, span] = (fourth + gains * signal).astype(BF16)
        flow.start(o_ref.at[:, span], results[0].at[:, span])


def add_body(flow, ins, results, outs):
    for n, out in enumerate(outs):
        span = slice(n * LANES, (n + 1) * LANES)
        out[...] = (ins[0][:, span].astype(F32) + ins[1][:, span].astype(F32)).astype(BF16)


def total_body(flow, ins, results, outs, scr):
    a_ref, b_ref = ins
    for k in range(ROWS):
        total = a_ref[k].astype(F32) + b_ref[k].astype(F32)
        scr[pl.ds(k, LANES, stride=ROWS), :] = total.T
    outs[0][...] = scr[...].astype(BF16)


def place(flow, chunk, blocks, whole):
    core = my_core()
    for owner, block in zip((core, 1 - core), blocks):
        start = pl.multiple_of(owner * HALF + chunk * LANES, LANES)
        flow.start(block, whole.at[:, pl.ds(start, LANES)])


def start_body(flow, ins, results, outs):
    place(flow, 0, ins, results[0])


def end_body(flow, ins, results, outs):
    place(flow, 1, ins[1:], results[0])


def gather_body(flow, ins, results, outs):
    for e, block in enumerate(ins):
        flow.start(block, results[0].at[:, e])


def spread_body(flow, ins, results, outs):
    for e, block in enumerate(outs):
        block[...] = ins[0][:, e]


def gathered(blocks):
    return call(
        gather_body, [Far(WHOLE)], [], *blocks, copies=Z_LO, weight_us=EXCHANGE_US
    )[0]


def scattered(whole):
    return call(spread_body, [BLOCK] * Z_LO, [], whole)


def across_z(blocks):
    moved = list(blocks)
    for e in range(1, Z_LO):
        moved[e] = lax.ppermute(
            blocks[e], "seq", [(i, i ^ (e * YX)) for i in range(Z_LO * YX)]
        )
    return moved


def tied(*values):
    return lax.optimization_barrier(values)


def across_yx(whole):
    groups = [[g * YX + t for t in range(YX)] for g in range(Z_LO)]
    return lax.all_to_all(
        whole, "seq", split_axis=0, concat_axis=0, axis_index_groups=groups, tiled=True
    )


def swap(block, bit):
    return lax.ppermute(block, "dp", [(i, i ^ bit) for i in range(4)])


def shards(
    inputs,
    grad_out,
    factor_one,
    factor_two,
    factor_three,
    factor_four,
    twiddle_in,
    twiddle_out,
    filter_freq,
    skip_gain,
):
    batch, chans, local_len = inputs.shape
    signal = inputs.reshape(chans, local_len)
    upstream = grad_out.reshape(chans, local_len)

    sent = call(
        first_body,
        [Far(WHOLE)],
        [SQUARE, TALL],
        factor_one,
        twiddle_in,
        signal,
        copies=Z_LO,
        weight_us=EXCHANGE_US,
    )[0]
    back = call(back_body, [BLOCK] * Z_LO, [SQUARE, TALL], Far(factor_four), Far(upstream))
    filt = jnp.transpose(filter_freq, (1, 2, 0))
    gains = skip_gain.reshape(chans, 1)
    moved, back_whole, filt, two, three, gains = tied(
        across_yx(sent),
        gathered(across_z(back)),
        filt,
        factor_two.T,
        factor_three.T,
        gains,
    )
    got = across_z(scattered(moved))
    back_got = across_yx(back_whole)

    spread, *mixed = call(
        middle_body,
        [Far(struct((ROWS, WIDTH, LANES)))] + [BLOCK] * Z_LO,
        [SQUARE, SQUARE] + [pltpu.VMEM((PAIRS, WIDTH, 2 * LANES), BF16)] * 2,
        Far(two),
        Far(twiddle_out),
        *got,
        Far(filt),
        Far(three),
        copies=PAIRS,
        weight_us=EXCHANGE_US,
    )
    half = struct((ROWS, HALF, LANES))
    keep, send = call(
        grad_body,
        [half, half],
        [SQUARE],
        Far(factor_three),
        Far(twiddle_out),
        back_got,
        Far(spread),
        weight_us=EXCHANGE_US,
    )
    mixed_whole = gathered(across_z(mixed))
    quarter = struct((ROWS, LANES, LANES))
    pairs = call(add_body, [quarter] * 2, [], keep, swap(send, 1))
    mixed_whole, pairs = tied(mixed_whole, pairs)
    returned = across_yx(mixed_whole)
    flat = struct((LANES * ROWS, LANES))
    far = [swap(pair, 2) for pair in pairs]
    outputs = call(
        last_body,
        [Far(struct((chans, local_len)))],
        [SQUARE, TALL],
        factor_four,
        gains,
        returned,
        signal,
        copies=ROWS,
    )[0]
    far[1], outputs = tied(far[1], outputs)
    mine = [
        call(total_body, [flat], [pltpu.VMEM(flat.shape, F32)], pair, got_far, weight_us=weight)[0]
        for pair, got_far, weight in zip(pairs, far, (0, 0))
    ]
    other = [swap(total, 1) for total in mine]
    whole = struct((LANES * ROWS, WIDTH))
    begun = call(start_body, [Far(whole)], [], mine[0], other[0], copies=2)[0]
    filter_grad = call(
        end_body,
        [Far(whole)],
        [],
        Far(begun),
        mine[1],
        other[1],
        copies=2,
        fetch=(),
        aliases={0: 0},
    )[0]
    return (
        outputs.reshape(batch, chans, local_len),
        filter_grad.reshape(chans, ROWS, WIDTH),
    )


def solution(mesh):
    in_specs = (
        P("dp", None, "seq"),
        P("dp", None, "seq"),
        P(),
        P(),
        P(),
        P(),
        P("seq", None),
        P("seq", None),
        P(None, "seq", None),
        P(),
    )
    out_specs = (P("dp", None, "seq"), P(None, "seq", None))
    return jax.shard_map(shards, mesh=mesh, in_specs=in_specs, out_specs=out_specs, check_vma=False)
```

```python
import jax
import jax.numpy as jnp
from jax import lax
from jax.experimental import pallas as pl
from jax.experimental.pallas import tpu as pltpu
from jax.sharding import PartitionSpec as P

F32 = jnp.float32
BF16 = jnp.bfloat16
LANES = 128
ROWS = 8
WIDTH = 512
HALF = WIDTH // 2
Z_LO = 4
YX = 16
PART = WIDTH // Z_LO
MSG = ROWS * ROWS
PAIRS = ROWS // 2
EXCHANGE_US = 60

NT = (((1,), (1,)), ((), ()))
NN = (((1,), (0,)), ((), ()))
TN = (((0,), (0,)), ((), ()))


def dot(left, right, dims=NN):
    return lax.dot_general(left, right, dims, preferred_element_type=F32)


def my_z():
    return lax.axis_index("seq") // YX


def my_core():
    return lax.axis_index("dp") % 2


def part(z, e):
    return pl.ds(pl.multiple_of((z ^ e) * PART, PART), PART)


def halves(core):
    return pl.ds(pl.multiple_of(core * HALF, HALF), HALF)


def struct(shape, dtype=BF16):
    return jax.ShapeDtypeStruct(shape, dtype)


BLOCK = struct((YX, MSG, LANES))
WHOLE = struct((YX, Z_LO, MSG, LANES))
SQUARE = pltpu.VMEM((WIDTH, WIDTH), BF16)
TALL = pltpu.VMEM((WIDTH * ROWS, LANES), F32)


class Copies:
    def __init__(self, sems):
        self.sems = sems
        self.started = []
        self.waited = set()
        self.inputs = {}

    def start(self, src, dst):
        copy = pltpu.make_async_copy(src, dst, self.sems.at[len(self.started)])
        copy.start()
        self.started.append(copy)

    def fetch(self, arg, src, dst):
        self.inputs[arg] = len(self.started)
        self.start(src, dst)

    def wait(self, *args):
        for arg in args:
            self.finish(self.inputs.get(arg))

    def finish(self, n):
        if n is not None and n not in self.waited:
            self.waited.add(n)
            self.started[n].wait()

    def finish_all(self):
        for n in range(len(self.started)):
            self.finish(n)


class Far:
    def __init__(self, value, pinned=True):
        self.value = value
        self.pinned = pinned


def call(body, outs, scratch, *args, copies=0, weight_us=0, fetch=None, aliases=None):
    n_in, n_out = len(args), len(outs)
    far_in = [n for n, a in enumerate(args) if isinstance(a, Far)]
    far_out = [n for n, o in enumerate(outs) if isinstance(o, Far)]
    pinned = [n for n in far_in if args[n].pinned]
    args = [a.value if isinstance(a, Far) else a for a in args]
    outs = [o.value if isinstance(o, Far) else o for o in outs]
    hbm = pl.BlockSpec(memory_space=pltpu.HBM)
    free = pl.BlockSpec(memory_space=pl.ANY)
    vmem = pl.BlockSpec(memory_space=pltpu.VMEM)

    def space(n):
        return hbm if n in pinned else free if n in far_in else vmem

    fetched = [n for n in far_in if fetch is None or n in fetch]

    def wrapped(*refs):
        refs = list(refs)
        ins, refs = refs[:n_in], refs[n_in:]
        results, refs = refs[:n_out], refs[n_out:]
        flow = Copies(refs.pop(0))
        for n in fetched:
            near = refs.pop(0)
            flow.fetch(n, ins[n], near)
            ins[n] = near
        near_results = list(results)
        for n in far_out:
            near_results[n] = refs.pop(0)
        body(flow, ins, results, near_results, *refs)
        flow.finish_all()

    return pl.pallas_call(
        wrapped,
        out_shape=[
            pltpu.HBM(o.shape, o.dtype) if n in far_out else o for n, o in enumerate(outs)
        ],
        in_specs=[space(n) for n in range(n_in)],
        out_specs=[hbm if n in far_out else vmem for n in range(n_out)],
        scratch_shapes=[pltpu.SemaphoreType.DMA((max(1, len(far_in) + copies),))]
        + [pltpu.VMEM(args[n].shape, args[n].dtype) for n in fetched]
        + [pltpu.VMEM(outs[n].shape, outs[n].dtype) for n in far_out]
        + scratch,
        input_output_aliases=aliases or {},
        compiler_params=pltpu.CompilerParams(vmem_limit_bytes=16 * 1024 * 1024),
        cost_estimate=pl.CostEstimate(
            flops=weight_us * 10**9, bytes_accessed=weight_us * 3 * 10**6, transcendentals=0
        ),
    )(
        *[
            pltpu.with_memory_space_constraint(a, pltpu.HBM) if n in pinned else a
            for n, a in enumerate(args)
        ]
    )


def rows_out(weight_scr, x_ref, twist, scr, finish):
    for pair in range(PAIRS):
        left = x_ref[:, (2 * pair) * WIDTH : (2 * pair + 1) * WIDTH]
        right = x_ref[:, (2 * pair + 1) * WIDTH : (2 * pair + 2) * WIDTH]
        both = dot(weight_scr[...], jnp.concatenate([left, right], axis=0), NT)
        for half in range(2):
            r = 2 * pair + half
            value = both[:, half * LANES : (half + 1) * LANES]
            if twist is not None:
                value = value * twist[:, r : r + 1]
            scr[pl.ds(r, WIDTH, stride=ROWS), :] = value
    step = WIDTH * ROWS // Z_LO
    for e in range(Z_LO):
        finish(e, scr[e * step : (e + 1) * step, :].astype(BF16).reshape(YX, MSG, LANES))


def first_body(flow, ins, results, outs, fscr, scr):
    f_ref, tw_ref, x_ref = ins
    z = my_z()
    flow.wait(0, 1)
    twist = []
    for e in range(Z_LO):
        fscr[e * PART : (e + 1) * PART, :] = f_ref[:, part(z, e)].T
        twist.append(tw_ref[:, part(z, e)].astype(F32).T)
    flow.wait(2)

    def finish(e, block):
        outs[0][:, e] = block
        flow.start(outs[0].at[:, e], results[0].at[:, e])

    rows_out(fscr, x_ref, jnp.concatenate(twist, axis=0), scr, finish)


def back_body(flow, ins, results, outs, fscr, scr):
    f_ref, x_ref = ins
    z = my_z()
    flow.wait(0)
    for e in range(Z_LO):
        fscr[e * PART : (e + 1) * PART, :] = f_ref[part(z, e), :]
    flow.wait(1)

    def finish(e, block):
        outs[e][...] = block

    rows_out(fscr, x_ref, None, scr, finish)


def columns(refs, pair):
    got = [[], []]
    for ref in refs:
        block = ref[:, pair * 16 : (pair + 1) * 16, :].astype(F32)
        block = block.reshape(YX, 2, ROWS, LANES)
        for half in range(2):
            got[half].append(block[:, half].reshape(PART, LANES))
    return [jnp.concatenate(parts, axis=0) for parts in got]


def twist_columns(tw_ref, z):
    return jnp.concatenate(
        [tw_ref[:, part(z, e)].astype(F32).T for e in range(Z_LO)], axis=0
    )


def middle_body(flow, ins, results, outs, f2s, f3s, cols_scr, mid_scr):
    f2t_ref, tw_ref, u0, u1, u2, u3, filt_ref, f3t_ref = ins
    zt_ref, *blocks = outs
    z = my_z()
    for pair in range(PAIRS):
        cols = columns((u0, u1, u2, u3), pair)
        for half in range(2):
            span = slice(half * LANES, (half + 1) * LANES)
            cols_scr[pair, :, span] = cols[half].astype(BF16)
    flow.wait(0)
    for e in range(Z_LO):
        f2s[:, e * PART : (e + 1) * PART] = f2t_ref[:, part(z, e)]
    for pair in range(PAIRS):
        k = 2 * pair
        spread = dot(f2s[...], cols_scr[pair]).astype(BF16)
        zt_ref[k] = spread[:, :LANES]
        zt_ref[k + 1] = spread[:, LANES:]
        flow.start(zt_ref.at[k : k + 2], results[0].at[k : k + 2])
        flow.wait(6)
        filt = jnp.concatenate([filt_ref[k], filt_ref[k + 1]], axis=1)
        mid_scr[pair] = (spread.astype(F32) * filt.astype(F32)).astype(BF16)
    flow.wait(1, 7)
    twist = twist_columns(tw_ref, z)
    for e in range(Z_LO):
        f3s[e * PART : (e + 1) * PART, :] = f3t_ref[part(z, e), :]
    for pair in range(PAIRS):
        k = 2 * pair
        third = dot(f3s[...], mid_scr[pair])
        first = third[:, :LANES] * twist[:, k : k + 1]
        second = third[:, LANES:] * twist[:, k + 1 : k + 2]
        shaped = jnp.concatenate(
            [first.reshape(Z_LO * YX, ROWS, LANES), second.reshape(Z_LO * YX, ROWS, LANES)],
            axis=1,
        ).astype(BF16)
        rows = slice(pair * 16, (pair + 1) * 16)
        for e, block in enumerate(blocks):
            block[:, rows, :] = shaped[e * YX : (e + 1) * YX]


def grad_body(flow, ins, results, outs, f3s, scr):
    f3_ref, tw_ref, d_ref, zt_ref = ins
    z = my_z()
    core = my_core()
    spans = (halves(core), halves(1 - core))
    flow.wait(0, 1)
    for n, span in enumerate(spans):
        for e in range(Z_LO):
            f3s[n * HALF : (n + 1) * HALF, e * PART : (e + 1) * PART] = f3_ref[span, part(z, e)]
    twist = twist_columns(tw_ref, z)
    for pair in range(PAIRS):
        k = 2 * pair
        cols = columns([d_ref.at[:, e] for e in range(Z_LO)], pair)
        rhs = jnp.concatenate(
            [(cols[h] * twist[:, k + h : k + h + 1]).astype(BF16) for h in range(2)], axis=1
        )
        grads = dot(f3s[...], rhs)
        flow.wait(3)
        for h in range(2):
            value = grads[:, h * LANES : (h + 1) * LANES]
            for n, span in enumerate(spans):
                spread = zt_ref[k + h, span, :].astype(F32)
                term = (spread * value[n * HALF : (n + 1) * HALF]).T
                for side in range(2):
                    scr[2 * n + side, pl.ds(k + h, LANES, stride=ROWS), :] = term[
                        :, side * LANES : (side + 1) * LANES
                    ]
    for n, out in enumerate(outs):
        for side in range(2):
            out[:, side * LANES : (side + 1) * LANES] = scr[2 * n + side].astype(BF16)


def last_body(flow, ins, results, outs, fscr, scr):
    f_ref, g_ref, s_ref, x_ref = ins
    o_ref = outs[0]
    z = my_z()
    step = YX * MSG
    for e in range(Z_LO):
        scr[e * step : (e + 1) * step, :] = s_ref[:, e].astype(F32).reshape(step, LANES)
    flow.wait(0)
    for e in range(Z_LO):
        fscr[e * PART : (e + 1) * PART, :] = f_ref[part(z, e), :]
    flow.wait(1, 3)
    gains = g_ref[...]
    for r in range(ROWS):
        rows = scr[pl.ds(r, WIDTH, stride=ROWS), :].astype(BF16)
        fourth = dot(rows, fscr[...], TN)
        span = slice(r * WIDTH, (r + 1) * WIDTH)
        signal = x_ref[:, span].astype(F32)
        o_ref[:, span] = (fourth + gains * signal).astype(BF16)
        flow.start(o_ref.at[:, span], results[0].at[:, span])


def add_body(flow, ins, results, outs):
    outs[0][...] = (ins[0][...].astype(F32) + ins[1][...].astype(F32)).astype(BF16)


def start_body(flow, ins, results, outs):
    flow.start(ins[0], results[0].at[:, halves(my_core())])


def end_body(flow, ins, results, outs):
    flow.start(ins[1], results[0].at[:, halves(1 - my_core())])


def gather_body(flow, ins, results, outs):
    for e, block in enumerate(ins):
        flow.start(block, results[0].at[:, e])


def spread_body(flow, ins, results, outs):
    for e, block in enumerate(outs):
        block[...] = ins[0][:, e]


def gathered(blocks):
    return call(
        gather_body, [Far(WHOLE)], [], *blocks, copies=Z_LO, weight_us=EXCHANGE_US
    )[0]


def scattered(whole):
    return call(spread_body, [BLOCK] * Z_LO, [], whole)


def across_z(blocks):
    moved = list(blocks)
    for e in range(1, Z_LO):
        moved[e] = lax.ppermute(
            blocks[e], "seq", [(i, i ^ (e * YX)) for i in range(Z_LO * YX)]
        )
    return moved


def tied(*values):
    return lax.optimization_barrier(values)


def across_yx(whole):
    groups = [[g * YX + t for t in range(YX)] for g in range(Z_LO)]
    return lax.all_to_all(
        whole, "seq", split_axis=0, concat_axis=0, axis_index_groups=groups, tiled=True
    )


def swap(block, bit):
    return lax.ppermute(block, "dp", [(i, i ^ bit) for i in range(4)])


def shards(
    inputs,
    grad_out,
    factor_one,
    factor_two,
    factor_three,
    factor_four,
    twiddle_in,
    twiddle_out,
    filter_freq,
    skip_gain,
):
    batch, chans, local_len = inputs.shape
    signal = inputs.reshape(chans, local_len)
    upstream = grad_out.reshape(chans, local_len)

    sent = call(
        first_body,
        [Far(WHOLE)],
        [SQUARE, TALL],
        factor_one,
        twiddle_in,
        signal,
        copies=Z_LO,
        weight_us=EXCHANGE_US,
    )[0]
    back = call(back_body, [BLOCK] * Z_LO, [SQUARE, TALL], Far(factor_four), Far(upstream))
    filt = jnp.transpose(filter_freq, (1, 2, 0))
    gains = skip_gain.reshape(chans, 1)
    moved, back_whole, filt, two, three, gains = tied(
        across_yx(sent),
        gathered(across_z(back)),
        filt,
        factor_two.T,
        factor_three.T,
        gains,
    )
    got = across_z(scattered(moved))
    back_got = across_yx(back_whole)

    spread, *mixed = call(
        middle_body,
        [Far(struct((ROWS, WIDTH, LANES)))] + [BLOCK] * Z_LO,
        [SQUARE, SQUARE] + [pltpu.VMEM((PAIRS, WIDTH, 2 * LANES), BF16)] * 2,
        Far(two),
        Far(twiddle_out),
        *got,
        Far(filt),
        Far(three),
        copies=PAIRS,
        weight_us=EXCHANGE_US,
    )
    half = struct((LANES * ROWS, HALF))
    keep, send = call(
        grad_body,
        [half, half],
        [SQUARE, pltpu.VMEM((4, LANES * ROWS, LANES), F32)],
        Far(factor_three),
        Far(twiddle_out),
        back_got,
        Far(spread),
        weight_us=EXCHANGE_US,
    )
    mixed_whole = gathered(across_z(mixed))
    pair = call(add_body, [half], [], keep, swap(send, 1))[0]
    mixed_whole, pair = tied(mixed_whole, pair)
    returned = across_yx(mixed_whole)
    far = swap(pair, 2)
    outputs = call(
        last_body,
        [Far(struct((chans, local_len)))],
        [SQUARE, TALL],
        factor_four,
        gains,
        returned,
        signal,
        copies=ROWS,
        weight_us=EXCHANGE_US,
    )[0]
    far, outputs = tied(far, outputs)
    whole = struct((LANES * ROWS, WIDTH))
    mine = call(add_body, [half], [], pair, far)[0]
    other = swap(mine, 1)
    begun = call(start_body, [Far(whole)], [], mine, copies=1)[0]
    filter_grad = call(
        end_body, [Far(whole)], [], Far(begun), other, copies=1, fetch=(), aliases={0: 0}
    )[0]
    return (
        outputs.reshape(batch, chans, local_len),
        filter_grad.reshape(chans, ROWS, WIDTH),
    )


def solution(mesh):
    in_specs = (
        P("dp", None, "seq"),
        P("dp", None, "seq"),
        P(),
        P(),
        P(),
        P(),
        P("seq", None),
        P("seq", None),
        P(None, "seq", None),
        P(),
    )
    out_specs = (P("dp", None, "seq"), P(None, "seq", None))
    return jax.shard_map(shards, mesh=mesh, in_specs=in_specs, out_specs=out_specs, check_vma=False)
```

```python
import jax
import jax.numpy as jnp
from jax import lax
from jax.experimental import pallas as pl
from jax.experimental.pallas import tpu as pltpu
from jax.sharding import PartitionSpec as P

F32 = jnp.float32
BF16 = jnp.bfloat16
LANES = 128
ROWS = 8
WIDTH = 512
HALF = WIDTH // 2
Z_LO = 4
YX = 16
OFFSETS = (0, 1, 3, 2)
PART = WIDTH // Z_LO
MSG = ROWS * ROWS
PAIRS = ROWS // 2
EXCHANGE_US = 60

NT = (((1,), (1,)), ((), ()))
NN = (((1,), (0,)), ((), ()))
TN = (((0,), (0,)), ((), ()))


def dot(left, right, dims=NN):
    return lax.dot_general(left, right, dims, preferred_element_type=F32)


def my_z():
    return lax.axis_index("seq") // YX


def my_core():
    return lax.axis_index("dp") % 2


def part(z, e):
    return pl.ds(pl.multiple_of((z ^ OFFSETS[e]) * PART, PART), PART)


def halves(core):
    return pl.ds(pl.multiple_of(core * HALF, HALF), HALF)


def struct(shape, dtype=BF16):
    return jax.ShapeDtypeStruct(shape, dtype)


BLOCK = struct((YX, MSG, LANES))
WHOLE = struct((YX, Z_LO, MSG, LANES))
SQUARE = pltpu.VMEM((WIDTH, WIDTH), BF16)
TALL = pltpu.VMEM((WIDTH * ROWS, LANES), F32)


class Copies:
    def __init__(self, sems):
        self.sems = sems
        self.started = []
        self.waited = set()
        self.inputs = {}

    def start(self, src, dst):
        copy = pltpu.make_async_copy(src, dst, self.sems.at[len(self.started)])
        copy.start()
        self.started.append(copy)

    def fetch(self, arg, src, dst):
        self.inputs[arg] = len(self.started)
        self.start(src, dst)

    def wait(self, *args):
        for arg in args:
            self.finish(self.inputs.get(arg))

    def finish(self, n):
        if n is not None and n not in self.waited:
            self.waited.add(n)
            self.started[n].wait()

    def finish_all(self):
        for n in range(len(self.started)):
            self.finish(n)


class Far:
    def __init__(self, value, pinned=True):
        self.value = value
        self.pinned = pinned


def call(body, outs, scratch, *args, copies=0, weight_us=0, fetch=None, aliases=None):
    n_in, n_out = len(args), len(outs)
    far_in = [n for n, a in enumerate(args) if isinstance(a, Far)]
    far_out = [n for n, o in enumerate(outs) if isinstance(o, Far)]
    pinned = [n for n in far_in if args[n].pinned]
    args = [a.value if isinstance(a, Far) else a for a in args]
    outs = [o.value if isinstance(o, Far) else o for o in outs]
    hbm = pl.BlockSpec(memory_space=pltpu.HBM)
    free = pl.BlockSpec(memory_space=pl.ANY)
    vmem = pl.BlockSpec(memory_space=pltpu.VMEM)

    def space(n):
        return hbm if n in pinned else free if n in far_in else vmem

    fetched = [n for n in far_in if fetch is None or n in fetch]

    def wrapped(*refs):
        refs = list(refs)
        ins, refs = refs[:n_in], refs[n_in:]
        results, refs = refs[:n_out], refs[n_out:]
        flow = Copies(refs.pop(0))
        for n in fetched:
            near = refs.pop(0)
            flow.fetch(n, ins[n], near)
            ins[n] = near
        near_results = list(results)
        for n in far_out:
            near_results[n] = refs.pop(0)
        body(flow, ins, results, near_results, *refs)
        flow.finish_all()

    return pl.pallas_call(
        wrapped,
        out_shape=[
            pltpu.HBM(o.shape, o.dtype) if n in far_out else o for n, o in enumerate(outs)
        ],
        in_specs=[space(n) for n in range(n_in)],
        out_specs=[hbm if n in far_out else vmem for n in range(n_out)],
        scratch_shapes=[pltpu.SemaphoreType.DMA((max(1, len(far_in) + copies),))]
        + [pltpu.VMEM(args[n].shape, args[n].dtype) for n in fetched]
        + [pltpu.VMEM(outs[n].shape, outs[n].dtype) for n in far_out]
        + scratch,
        input_output_aliases=aliases or {},
        compiler_params=pltpu.CompilerParams(vmem_limit_bytes=16 * 1024 * 1024),
        cost_estimate=pl.CostEstimate(
            flops=weight_us * 10**9, bytes_accessed=weight_us * 3 * 10**6, transcendentals=0
        ),
    )(
        *[
            pltpu.with_memory_space_constraint(a, pltpu.HBM) if n in pinned else a
            for n, a in enumerate(args)
        ]
    )


def rows_out(weight_scr, x_ref, twist, scr, finish):
    for pair in range(PAIRS):
        left = x_ref[:, (2 * pair) * WIDTH : (2 * pair + 1) * WIDTH]
        right = x_ref[:, (2 * pair + 1) * WIDTH : (2 * pair + 2) * WIDTH]
        both = dot(weight_scr[...], jnp.concatenate([left, right], axis=0), NT)
        for half in range(2):
            r = 2 * pair + half
            value = both[:, half * LANES : (half + 1) * LANES]
            if twist is not None:
                value = value * twist[:, r : r + 1]
            scr[pl.ds(r, WIDTH, stride=ROWS), :] = value
    step = WIDTH * ROWS // Z_LO
    for e in range(Z_LO):
        finish(e, scr[e * step : (e + 1) * step, :].astype(BF16).reshape(YX, MSG, LANES))


def first_body(flow, ins, results, outs, fscr, scr):
    f_ref, tw_ref, x_ref = ins
    z = my_z()
    flow.wait(0, 1)
    twist = []
    for e in range(Z_LO):
        fscr[e * PART : (e + 1) * PART, :] = f_ref[:, part(z, e)].T
        twist.append(tw_ref[:, part(z, e)].astype(F32).T)
    flow.wait(2)

    def finish(e, block):
        outs[0][:, e] = block
        flow.start(outs[0].at[:, e], results[0].at[:, e])

    rows_out(fscr, x_ref, jnp.concatenate(twist, axis=0), scr, finish)


def back_body(flow, ins, results, outs, fscr, scr):
    f_ref, x_ref = ins
    z = my_z()
    flow.wait(0)
    for e in range(Z_LO):
        fscr[e * PART : (e + 1) * PART, :] = f_ref[part(z, e), :]
    flow.wait(1)

    def finish(e, block):
        outs[e][...] = block

    rows_out(fscr, x_ref, None, scr, finish)


def columns(refs, pair):
    got = [[], []]
    for ref in refs:
        block = ref[:, pair * 16 : (pair + 1) * 16, :].astype(F32)
        block = block.reshape(YX, 2, ROWS, LANES)
        for half in range(2):
            got[half].append(block[:, half].reshape(PART, LANES))
    return [jnp.concatenate(parts, axis=0) for parts in got]


def twist_columns(tw_ref, z):
    return jnp.concatenate(
        [tw_ref[:, part(z, e)].astype(F32).T for e in range(Z_LO)], axis=0
    )


def middle_body(flow, ins, results, outs, f2s, f3s, cols_scr, mid_scr):
    f2t_ref, tw_ref, u0, u1, u2, u3, filt_ref, f3t_ref = ins
    zt_ref, *blocks = outs
    z = my_z()
    for pair in range(PAIRS):
        cols = columns((u0, u1, u2, u3), pair)
        for half in range(2):
            span = slice(half * LANES, (half + 1) * LANES)
            cols_scr[pair, :, span] = cols[half].astype(BF16)
    flow.wait(0)
    for e in range(Z_LO):
        f2s[:, e * PART : (e + 1) * PART] = f2t_ref[:, part(z, e)]
    for pair in range(PAIRS):
        k = 2 * pair
        spread = dot(f2s[...], cols_scr[pair]).astype(BF16)
        zt_ref[k] = spread[:, :LANES]
        zt_ref[k + 1] = spread[:, LANES:]
        flow.start(zt_ref.at[k : k + 2], results[0].at[k : k + 2])
        flow.wait(6)
        filt = jnp.concatenate([filt_ref[k], filt_ref[k + 1]], axis=1)
        mid_scr[pair] = (spread.astype(F32) * filt.astype(F32)).astype(BF16)
    flow.wait(1, 7)
    twist = twist_columns(tw_ref, z)
    for e in range(Z_LO):
        f3s[e * PART : (e + 1) * PART, :] = f3t_ref[part(z, e), :]
    for pair in range(PAIRS):
        k = 2 * pair
        third = dot(f3s[...], mid_scr[pair])
        first = third[:, :LANES] * twist[:, k : k + 1]
        second = third[:, LANES:] * twist[:, k + 1 : k + 2]
        shaped = jnp.concatenate(
            [first.reshape(Z_LO * YX, ROWS, LANES), second.reshape(Z_LO * YX, ROWS, LANES)],
            axis=1,
        ).astype(BF16)
        rows = slice(pair * 16, (pair + 1) * 16)
        for e, block in enumerate(blocks):
            block[:, rows, :] = shaped[e * YX : (e + 1) * YX]


def grad_body(flow, ins, results, outs, f3s, scr):
    f3_ref, tw_ref, d_ref, zt_ref = ins
    z = my_z()
    core = my_core()
    spans = (halves(core), halves(1 - core))
    flow.wait(0, 1)
    for n, span in enumerate(spans):
        for e in range(Z_LO):
            f3s[n * HALF : (n + 1) * HALF, e * PART : (e + 1) * PART] = f3_ref[span, part(z, e)]
    twist = twist_columns(tw_ref, z)
    for pair in range(PAIRS):
        k = 2 * pair
        cols = columns([d_ref.at[:, e] for e in range(Z_LO)], pair)
        rhs = jnp.concatenate(
            [(cols[h] * twist[:, k + h : k + h + 1]).astype(BF16) for h in range(2)], axis=1
        )
        grads = dot(f3s[...], rhs)
        flow.wait(3)
        for h in range(2):
            value = grads[:, h * LANES : (h + 1) * LANES]
            for n, span in enumerate(spans):
                spread = zt_ref[k + h, span, :].astype(F32)
                term = (spread * value[n * HALF : (n + 1) * HALF]).T
                for side in range(2):
                    scr[2 * n + side, pl.ds(k + h, LANES, stride=ROWS), :] = term[
                        :, side * LANES : (side + 1) * LANES
                    ]
    for n, out in enumerate(outs):
        for side in range(2):
            out[:, side * LANES : (side + 1) * LANES] = scr[2 * n + side].astype(BF16)


def last_body(flow, ins, results, outs, fscr, scr):
    f_ref, g_ref, s_ref, x_ref = ins
    o_ref = outs[0]
    z = my_z()
    step = YX * MSG
    for e in range(Z_LO):
        scr[e * step : (e + 1) * step, :] = s_ref[:, e].astype(F32).reshape(step, LANES)
    flow.wait(0)
    for e in range(Z_LO):
        fscr[e * PART : (e + 1) * PART, :] = f_ref[part(z, e), :]
    flow.wait(1, 3)
    gains = g_ref[...]
    for r in range(ROWS):
        rows = scr[pl.ds(r, WIDTH, stride=ROWS), :].astype(BF16)
        fourth = dot(rows, fscr[...], TN)
        span = slice(r * WIDTH, (r + 1) * WIDTH)
        signal = x_ref[:, span].astype(F32)
        o_ref[:, span] = (fourth + gains * signal).astype(BF16)
        flow.start(o_ref.at[:, span], results[0].at[:, span])


def add_body(flow, ins, results, outs):
    outs[0][...] = (ins[0][...].astype(F32) + ins[1][...].astype(F32)).astype(BF16)


def start_body(flow, ins, results, outs):
    flow.start(ins[0], results[0].at[:, halves(my_core())])


def end_body(flow, ins, results, outs):
    flow.start(ins[1], results[0].at[:, halves(1 - my_core())])


def gather_body(flow, ins, results, outs):
    for e, block in enumerate(ins):
        flow.start(block, results[0].at[:, e])


def spread_body(flow, ins, results, outs):
    for e, block in enumerate(outs):
        block[...] = ins[0][:, e]


def gathered(blocks):
    return call(
        gather_body, [Far(WHOLE)], [], *blocks, copies=Z_LO, weight_us=EXCHANGE_US
    )[0]


def scattered(whole):
    return call(spread_body, [BLOCK] * Z_LO, [], whole)


def across_z(blocks):
    moved = list(blocks)
    for e in range(1, Z_LO):
        moved[e] = lax.ppermute(
            blocks[e], "seq", [(i, i ^ (OFFSETS[e] * YX)) for i in range(Z_LO * YX)]
        )
    return moved


def tied(*values):
    return lax.optimization_barrier(values)


def across_yx(whole):
    groups = [[g * YX + t for t in range(YX)] for g in range(Z_LO)]
    return lax.all_to_all(
        whole, "seq", split_axis=0, concat_axis=0, axis_index_groups=groups, tiled=True
    )


def swap(block, bit):
    return lax.ppermute(block, "dp", [(i, i ^ bit) for i in range(4)])


def shards(
    inputs,
    grad_out,
    factor_one,
    factor_two,
    factor_three,
    factor_four,
    twiddle_in,
    twiddle_out,
    filter_freq,
    skip_gain,
):
    batch, chans, local_len = inputs.shape
    signal = inputs.reshape(chans, local_len)
    upstream = grad_out.reshape(chans, local_len)

    sent = call(
        first_body,
        [Far(WHOLE)],
        [SQUARE, TALL],
        factor_one,
        twiddle_in,
        signal,
        copies=Z_LO,
        weight_us=EXCHANGE_US,
    )[0]
    back = call(back_body, [BLOCK] * Z_LO, [SQUARE, TALL], Far(factor_four), Far(upstream))
    filt = jnp.transpose(filter_freq, (1, 2, 0))
    gains = skip_gain.reshape(chans, 1)
    moved, back_whole, filt, two, three, gains = tied(
        across_yx(sent),
        gathered(across_z(back)),
        filt,
        factor_two.T,
        factor_three.T,
        gains,
    )
    got = across_z(scattered(moved))
    back_got = across_yx(back_whole)

    spread, *mixed = call(
        middle_body,
        [Far(struct((ROWS, WIDTH, LANES)))] + [BLOCK] * Z_LO,
        [SQUARE, SQUARE] + [pltpu.VMEM((PAIRS, WIDTH, 2 * LANES), BF16)] * 2,
        Far(two),
        Far(twiddle_out),
        *got,
        Far(filt),
        Far(three),
        copies=PAIRS,
        weight_us=EXCHANGE_US,
    )
    half = struct((LANES * ROWS, HALF))
    keep, send = call(
        grad_body,
        [half, half],
        [SQUARE, pltpu.VMEM((4, LANES * ROWS, LANES), F32)],
        Far(factor_three),
        Far(twiddle_out),
        back_got,
        Far(spread),
        weight_us=EXCHANGE_US,
    )
    mixed_whole = gathered(across_z(mixed))
    pair = call(add_body, [half], [], keep, swap(send, 1))[0]
    mixed_whole, pair = tied(mixed_whole, pair)
    returned = across_yx(mixed_whole)
    far = swap(pair, 2)
    outputs = call(
        last_body,
        [Far(struct((chans, local_len)))],
        [SQUARE, TALL],
        factor_four,
        gains,
        returned,
        signal,
        copies=ROWS,
        weight_us=EXCHANGE_US,
    )[0]
    far, outputs = tied(far, outputs)
    whole = struct((LANES * ROWS, WIDTH))
    mine = call(add_body, [half], [], pair, far)[0]
    other = swap(mine, 1)
    begun = call(start_body, [Far(whole)], [], mine, copies=1)[0]
    filter_grad = call(
        end_body, [Far(whole)], [], Far(begun), other, copies=1, fetch=(), aliases={0: 0}
    )[0]
    return (
        outputs.reshape(batch, chans, local_len),
        filter_grad.reshape(chans, ROWS, WIDTH),
    )


def solution(mesh):
    in_specs = (
        P("dp", None, "seq"),
        P("dp", None, "seq"),
        P(),
        P(),
        P(),
        P(),
        P("seq", None),
        P("seq", None),
        P(None, "seq", None),
        P(),
    )
    out_specs = (P("dp", None, "seq"), P(None, "seq", None))
    return jax.shard_map(shards, mesh=mesh, in_specs=in_specs, out_specs=out_specs, check_vma=False)
```
